32 devices in a mesh: parts: 2 (over y), outer: 2 (over core), expert: 4 (over z), inner: 2 (over x).
Axes of the slice: x: 2, y: 2, z: 4, core: 2. Of those that a mesh axis runs over, the one named last changes fastest.
Arguments:
- tokens: bfloat16 [2048, 4096], P(('parts', 'outer', 'expert'), 'inner'), parts along dimension 0, may hold values from -6 to 6
- expert_ids: int32 [2048, 8], P(('parts', 'outer', 'expert')), parts along dimension 0, may hold values from 0 to 127, all different within a row; in each aligned block of 128 rows (0 to 127, 128 to 255, ...) at most 16 rows name the same one
- gate_num: int32 [2048, 8], P(('parts', 'outer', 'expert')), parts along dimension 0, may hold values from 1 to 64
- gate_weight: bfloat16 [8, 4096, 1536], P(('outer', 'expert'), None, 'inner'), may hold values from -0.09375 to 0.09375
- up_weight: bfloat16 [8, 4096, 1536], P(('outer', 'expert'), None, 'inner'), may hold values from -0.09375 to 0.09375
- down_weight: bfloat16 [8, 1536, 4096], P(('outer', 'expert'), None, 'inner'), may hold values from -0.15625 to 0.15625
Outputs:
- mixed: bfloat16 [2048, 4096], P(('parts', 'outer', 'expert'), 'inner'), parts along dimension 0
The draws below stay inside these ranges and needn't reach their ends.
There are 2 independent parts, one for each index of `parts`. The reference program is written for one: setup_inputs(seed, part) draws one part's arguments, and reference() takes and returns one part's arrays. A program takes and returns all parts, laid end to end along the dimension named above; an argument that names none is the same for every part. Nothing has to cross between parts.
Inputs may be any that keep to these rules, and one draw needn't show every extreme that they name: `expert_ids`: each row names 8 different experts. In each aligned block of 128 rows (the tokens of one group), no expert is named by more than 16 rows, a bound that some block reaches.
All inputs are finite; a program needn't handle non-finite values.
Results may differ from the reference program's by a relative error of at most 0.0057.
Values may be sent and summed in bfloat16 or wider, within the bound.
No kernel may reach another device: no remote copies, remote signals or barrier semaphores. Data moves between devices by JAX's collectives and lax.ppermute only.
A program may use at most 64 MiB of HBM per device.

```python
import math
import jax
import jax.numpy as jnp
import numpy as np
from jax import lax

D = 4096
FF = 1536
EXPERTS = 128
TOPK = 8
TOK_GRP = 128
CAP = 16
EXP_WIN = 8
TOKENS = 1024
N_OUTER = 2
N_EXPERT = 4


def plant(entries, stream_key, low, largest):
    extent = entries.shape
    index_at = [jax.random.randint(jax.random.fold_in(stream_key, axis), (), 0, extent[axis]) for axis in range(len(extent))]
    entries = entries.at[tuple(index_at)].set(low)
    longest = extent.index(max(extent))
    index_at[longest] = (index_at[longest] + 1) % extent[longest]
    return entries.at[tuple(index_at)].set(largest)


def steps_of(key, shape, shards, low, top_value):
    def one(axis_at, blocks):
        heights = jax.random.uniform(jax.random.fold_in(jax.random.fold_in(key, 6), axis_at), (blocks,), jnp.float32, low / len(shards), top_value / len(shards))
        return jnp.repeat(jnp.exp(heights), shape[axis_at] // blocks).reshape((-1,) + (1,) * (len(shape) - axis_at - 1))

    gain = one(*shards[0])
    for cut in shards[1:]:
        gain = gain * one(*cut)
    return gain


def shared_out(stream_key, own, number, rows, amount, top, bound, lean):
    ranking = jax.random.permutation(stream_key, amount)
    crowded, common = load_shares(amount, rows * top, bound, lean, True), load_shares(amount, rows * top, bound, lean, False)
    places = jnp.arange(amount)

    def named(tallies, rotation):
        used = int((tallies > 0).sum())
        fixed = max(1, used // 4)
        shifted = fixed + (places - fixed + rotation * (used - fixed)) % max(1, amount - fixed)
        return jnp.zeros((amount,), jnp.int32).at[ranking[jnp.where(places < fixed, places, shifted)]].set(jnp.asarray(tallies, jnp.int32))

    tallies = jnp.where(number % 4 == 0, named(crowded, number // 4), named(common, number - number // 4 - 1))
    mixed = jax.random.permutation(jax.random.fold_in(own, 3), amount)
    source_of, taker = mixed[0:amount // 2 * 2:2], mixed[1:amount // 2 * 2:2]
    slack = jnp.minimum(tallies[source_of] - 1, bound - tallies[taker]) // 2
    slack = jnp.where((source_of == ranking[0]) | (taker == ranking[0]) | (tallies[taker] == 0), 0, jnp.maximum(slack, 0))
    shifted = jax.random.randint(jax.random.fold_in(own, 4), (amount // 2,), 0, 1 << 20) % (slack + 1)
    tallies = tallies.at[source_of].add(-shifted).at[taker].add(shifted)
    labels = jnp.searchsorted(jnp.cumsum(tallies), jnp.arange(rows * top), side="right").astype(jnp.int32)
    table = labels.reshape(top, rows).T
    table = table[jax.random.permutation(jax.random.fold_in(own, 1), rows)]
    rotation = jax.random.randint(jax.random.fold_in(own, 2), (rows, 1), 0, top)
    return jnp.take_along_axis(table, (jnp.arange(top)[None, :] + rotation) % top, axis=1)


def load_shares(number_of, total, limit, slope, full):
    loads = [(1 << 20) // math.isqrt(grade ** slope) + 1 for grade in range(1, number_of + 1)]
    largest = limit if full else min(limit, max(-(-total // number_of), total * loads[0] // sum(loads)))
    least = 1 if total - largest >= number_of - 1 else 0
    given, spare = [largest] + [least] * (number_of - 1), total - largest - least * (number_of - 1)
    while spare > 0:
        candidates = [i for i in range(1, number_of) if given[i] < largest] or [i for i in range(1, number_of) if given[i] < limit]
        whole, budget = sum([loads[i] for i in candidates]), spare
        for i in candidates:
            more = min(limit - given[i], max(1, budget * loads[i] // whole), spare)
            given[i] = given[i] + more
            spare = spare - more
    return np.array(given)


def normal_values(key, dims, width, bound, split=(), kind=jnp.bfloat16):
    loudness = steps_of(key, dims, split, -0.22, 0.18) if split else 1.0
    values = jax.random.normal(key, dims, jnp.float32) * width * loudness
    return jnp.minimum(jnp.maximum(values, -bound), bound).astype(kind)


def setup_inputs(seed: int = 0, part: int = 0) -> dict:
    keys = jax.random.split(jax.random.key(seed), 7)
    part_splits = jax.random.split(jax.random.fold_in(keys[6], part), 7)
    tokens = normal_values(part_splits[0], (TOKENS, D), 1.0, 6.0, ((0, 8), (1, 2)))
    expert_ids_keys = jax.random.split(jax.random.fold_in(part_splits[1], 1), TOKENS // TOK_GRP)
    expert_ids_turns = jax.random.permutation(jax.random.fold_in(part_splits[1], 3), TOKENS // TOK_GRP)
    expert_ids = jax.vmap(lambda own, number: shared_out(jax.random.fold_in(part_splits[1], 2), own, number, TOK_GRP, EXPERTS, TOPK, CAP, 2))(expert_ids_keys, expert_ids_turns).reshape((TOKENS, TOPK))
    gate_num = plant(jax.random.randint(part_splits[2], (TOKENS, TOPK), 1, 65), jax.random.fold_in(part_splits[2], 1), 1, 64).astype(jnp.int32)
    gate_weight = normal_values(keys[3], (EXP_WIN, D, FF), D ** -0.5, 0.09375, ((0, 8), (2, 2)))
    up_weight = normal_values(keys[4], (EXP_WIN, D, FF), D ** -0.5, 0.09375, ((0, 8), (2, 2)))
    down_weight = normal_values(keys[5], (EXP_WIN, FF, D), FF ** -0.5, 0.15625, ((0, 8), (2, 2)))
    return dict(tokens=tokens, expert_ids=expert_ids, gate_num=gate_num, gate_weight=gate_weight, up_weight=up_weight, down_weight=down_weight)


def reference(tokens, expert_ids, gate_num, gate_weight, up_weight, down_weight):
    groups = N_OUTER * N_EXPERT
    token_count = tokens.shape[0]
    is_live = expert_ids < groups
    numerators = jnp.where(is_live, gate_num, 0).astype(jnp.float32)
    weight = numerators / jnp.maximum(jnp.sum(numerators, axis=1, keepdims=True), 1.0)
    selected = (expert_ids[:, :, None] == jnp.arange(groups, dtype=jnp.int32)[None, None, :]).astype(jnp.int32)
    per_token = jnp.sum(selected, axis=1).reshape(groups, TOK_GRP, groups)
    earlier = (jnp.cumsum(per_token, axis=1) - per_token).reshape(token_count, groups)
    slot_index = jnp.sum(selected * earlier[:, None, :], axis=2)
    group_index = (jnp.arange(token_count, dtype=jnp.int32) // TOK_GRP)[:, None]
    dump_row = groups * groups * CAP
    place_index = jnp.where(is_live, expert_ids * (groups * CAP) + group_index * CAP + slot_index, dump_row).astype(jnp.int32)
    token_ids = jnp.broadcast_to(jnp.arange(token_count, dtype=jnp.int32)[:, None], place_index.shape)
    slot_tokens = jnp.full((dump_row + 1,), token_count, jnp.int32).at[place_index.reshape(-1)].set(token_ids.reshape(-1))
    slot_tokens = slot_tokens[:dump_row].reshape(groups, groups * CAP)
    slot_weights = jnp.zeros((dump_row + 1,), weight.dtype).at[place_index.reshape(-1)].set(weight.reshape(-1))
    slot_weights = slot_weights[:dump_row].reshape(groups, groups * CAP)
    padded = jnp.concatenate([tokens, jnp.zeros((1, D), tokens.dtype)], axis=0)

    def expert_step(accum, step_inputs):
        row_index, row_weight, gate_matrix, up_matrix, down_matrix = step_inputs
        routed = padded[row_index]
        gate_proj = jnp.dot(routed, gate_matrix, preferred_element_type=jnp.float32)
        up_proj = jnp.dot(routed, up_matrix, preferred_element_type=jnp.float32)
        hidden = (jax.nn.silu(gate_proj) * up_proj).astype(jnp.bfloat16)
        expert_out = jnp.dot(hidden, down_matrix, preferred_element_type=jnp.float32).astype(jnp.bfloat16)
        accum = accum.at[row_index].add(row_weight[:, None] * expert_out.astype(jnp.float32), mode="drop")
        return accum, None

    mixed_out, _ = lax.scan(expert_step, jnp.zeros((token_count, D), jnp.float32), (slot_tokens, slot_weights, gate_weight, up_weight, down_weight))
    return mixed_out.astype(jnp.bfloat16)
```

```python
import functools

import jax
import jax.numpy as jnp
from jax import lax
from jax.experimental import pallas as pl
from jax.experimental.pallas import tpu as pltpu
from jax.sharding import PartitionSpec as P

CAP = 16
MIB = 1 << 20
VMEM = pl.BlockSpec(memory_space=pltpu.VMEM)
SMEM = pl.BlockSpec(memory_space=pltpu.SMEM)
BF16, F32 = jnp.bfloat16, jnp.float32


def call(body, outs, specs, cost, limit=16):
    flops, moved = cost
    return pl.pallas_call(
        body,
        out_shape=[jax.ShapeDtypeStruct(s, d) for s, d in outs],
        in_specs=specs,
        out_specs=[VMEM] * len(outs),
        compiler_params=pltpu.CompilerParams(vmem_limit_bytes=limit * MIB),
        cost_estimate=pl.CostEstimate(flops=flops, bytes_accessed=moved, transcendentals=0),
    )


def turn(x, axis, by):
    size = lax.axis_size(axis)
    return lax.ppermute(x, axis, [(k, (k + by) % size) for k in range(size)])


def spread(order):
    steps = []
    for k in range(1, order):
        for step in (k, order - k):
            if step not in steps and 0 < step < order:
                steps.append(step)
    return steps


def hits_of(order_ref, ids, groups):
    rows = [
        jnp.max(jnp.where(ids == order_ref[j], 1.0, 0.0), axis=0, keepdims=True)
        for j in range(groups)
    ]
    return jnp.concatenate(rows, axis=0)


def places(hits):
    groups, count = hits.shape
    before = lax.broadcasted_iota(jnp.int32, (count, count), 0)
    after = lax.broadcasted_iota(jnp.int32, (count, count), 1)
    earlier = jnp.dot(
        hits.astype(BF16),
        jnp.where(before < after, 1.0, 0.0).astype(BF16),
        preferred_element_type=F32,
    )
    slot = lax.broadcasted_iota(jnp.int32, (groups, CAP, count), 1).astype(F32)
    taken = jnp.where(hits > 0.5, earlier, -1.0)
    return jnp.where(taken[:, None, :] == slot, 1.0, 0.0)


def fill_kernel(groups, parts, order_ref, ids_ref, tokens_ref, *outs):
    pick = places(hits_of(order_ref, ids_ref[...], groups))
    pick = pick.reshape(groups * CAP, ids_ref.shape[1]).astype(BF16)
    rows = jnp.dot(pick, tokens_ref[...], preferred_element_type=F32).astype(BF16)
    at = 0
    for out, size in zip(outs, parts):
        out[...] = rows[at : at + size]
        at += size


def share_kernel(groups, order_ref, ids_ref, num_ref, high_ref, low_ref):
    ids = ids_ref[...]
    count = ids.shape[1]
    num = num_ref[...].astype(F32)
    live = jnp.where(ids < groups, num, 0.0)
    total = jnp.maximum(jnp.sum(live, axis=0, keepdims=True), 1.0)
    given = [
        jnp.sum(jnp.where(ids == order_ref[j], num, 0.0), axis=0, keepdims=True) / total
        for j in range(groups)
    ]
    weight = jnp.concatenate(given, axis=0)
    slots = places(hits_of(order_ref, ids, groups)) * weight[:, None, :]
    mix = slots.reshape(groups * CAP, count).T
    high = mix.astype(BF16)
    high_ref[...] = high
    low_ref[...] = (mix - high.astype(F32)).astype(BF16)


def rows_of(refs):
    return jnp.concatenate([r[...] for r in refs], axis=0)


def in_first_kernel(n, at_ref, *refs):
    x, (gate_ref, up_ref, g_ref, u_ref) = rows_of(refs[:n]), refs[n:]
    depth = x.shape[1]
    at = pl.ds(pl.multiple_of(at_ref[0] * depth, depth), depth)
    g_ref[...] = jnp.dot(x, gate_ref[0, at, :], preferred_element_type=F32)
    u_ref[...] = jnp.dot(x, up_ref[0, at, :], preferred_element_type=F32)


def in_last_kernel(n, peers, at_ref, *refs):
    xs, (gate_ref, up_ref, g_ref, u_ref, h_ref) = refs[: n * peers], refs[n * peers :]
    g, u = g_ref[...], u_ref[...]
    for p in range(peers):
        x = rows_of(xs[p * n : (p + 1) * n])
        depth = x.shape[1]
        at = pl.ds(pl.multiple_of(at_ref[p] * depth, depth), depth)
        g += jnp.dot(x, gate_ref[0, at, :], preferred_element_type=F32)
        u += jnp.dot(x, up_ref[0, at, :], preferred_element_type=F32)
    h_ref[...] = (g * jax.nn.sigmoid(g) * u).astype(BF16)


def out_first_kernel(at_ref, h_ref, down_ref, o_ref):
    depth = h_ref.shape[1]
    at = pl.ds(pl.multiple_of(at_ref[0] * depth, depth), depth)
    o_ref[...] = jnp.dot(h_ref[...], down_ref[0, at, :], preferred_element_type=F32)


def out_last_kernel(peers, at_ref, *refs):
    hs, (down_ref, o_ref), outs = refs[:peers], refs[peers : peers + 2], refs[peers + 2 :]
    total = o_ref[...]
    for p in range(peers):
        depth = hs[p].shape[1]
        at = pl.ds(pl.multiple_of(at_ref[p] * depth, depth), depth)
        total += jnp.dot(hs[p][...], down_ref[0, at, :], preferred_element_type=F32)
    size = outs[0].shape[0]
    for k, out in enumerate(outs):
        out[...] = total[k * size : (k + 1) * size].astype(BF16)


def mix_kernel(high_ref, low_ref, *refs):
    rows, out_ref = rows_of(refs[:-1]), refs[-1]
    total = jnp.dot(high_ref[...], rows, preferred_element_type=F32)
    total += jnp.dot(low_ref[...], rows, preferred_element_type=F32)
    out_ref[...] = total.astype(BF16)


def local(tokens, expert_ids, gate_num, gate_weight, up_weight, down_weight):
    cores, depths, peers = (lax.axis_size(a) for a in ("outer", "expert", "inner"))
    core, depth, side = (lax.axis_index(a) for a in ("outer", "expert", "inner"))
    groups = cores * depths
    count, width = tokens.shape
    hidden_size = gate_weight.shape[2]
    out_width = down_weight.shape[2]
    total = groups * CAP
    order = jnp.stack(
        [
            lax.rem(core + c, cores) * depths + lax.rem(depth + s, depths)
            for c in range(cores)
            for s in range(depths)
        ]
    ).astype(jnp.int32)
    ids, num = expert_ids.T, gate_num.T

    parts = [CAP] * depths + [depths * CAP] * (cores - 1)
    sent = call(
        functools.partial(fill_kernel, groups, parts),
        [((p, width), BF16) for p in parts],
        [SMEM, VMEM, VMEM],
        (2 * total * count * width, 4 * total * width),
    )(order, ids, tokens)
    traded = [turn(sent[depths + c - 1], "outer", c) for c in range(1, cores)]
    chunks = [
        jnp.concatenate([sent[s]] + [t[s * CAP : (s + 1) * CAP] for t in traded], axis=0)
        for s in range(depths)
    ]
    steps = spread(depths)
    here = [chunks[0]] + [turn(chunks[s], "expert", s) for s in steps]
    if depths > 4 or peers > 2:
        here = [jnp.concatenate(here, axis=0)]
    there = [[turn(x, "inner", p) for x in here] for p in range(1, peers)]

    high, low = call(
        functools.partial(share_kernel, groups),
        [((count, total), BF16)] * 2,
        [SMEM, VMEM, VMEM],
        (2 * groups * count * count, 4 * total * count),
    )(order, ids, num)

    mine = side.reshape(1).astype(jnp.int32)
    others = jnp.stack([lax.rem(side + peers - p, peers) for p in range(1, peers)]).astype(jnp.int32)
    n = len(here)
    flops = 4 * total * width * hidden_size
    g, u = call(
        functools.partial(in_first_kernel, n),
        [((total, hidden_size), F32)] * 2,
        [SMEM] + [VMEM] * (n + 2),
        (flops, 4 * width * hidden_size),
        28,
    )(mine, *here, gate_weight, up_weight)
    (hidden,) = call(
        functools.partial(in_last_kernel, n, peers - 1),
        [((total, hidden_size), BF16)],
        [SMEM] + [VMEM] * (n * (peers - 1) + 4),
        (flops * (peers - 1), 4 * width * hidden_size * (peers - 1)),
        28,
    )(others, *[x for xs in there for x in xs], gate_weight, up_weight, g, u)
    hidden_there = [turn(hidden, "inner", p) for p in range(1, peers)]
    flops = 2 * total * hidden_size * out_width
    (partial,) = call(
        out_first_kernel,
        [((total, out_width), F32)],
        [SMEM, VMEM, VMEM],
        (flops, 2 * hidden_size * out_width),
        20,
    )(mine, hidden, down_weight)
    done = call(
        functools.partial(out_last_kernel, peers - 1),
        [((cores * CAP, out_width), BF16)] * depths,
        [SMEM] + [VMEM] * (peers + 1),
        (flops * (peers - 1), 2 * hidden_size * out_width * (peers - 1)),
        20,
    )(others, *hidden_there, down_weight, partial)

    back = {0: done[0]}
    for k, s in enumerate(steps):
        back[s] = turn(done[k + 1], "expert", depths - s)
    final = [back[s][:CAP] for s in range(depths)]
    for c in range(1, cores):
        for s in range(depths):
            final.append(turn(back[s][c * CAP : (c + 1) * CAP], "outer", cores - c))
    (mixed,) = call(
        mix_kernel,
        [((count, out_width), BF16)],
        [VMEM] * (2 + len(final)),
        (4 * count * total * out_width, 4 * count * out_width),
    )(high, low, *final)
    return mixed


def solution(mesh):
    placed = (
        P(("parts", "outer", "expert"), "inner"),
        P(("parts", "outer", "expert"), None),
        P(("parts", "outer", "expert"), None),
        P(("outer", "expert"), None, "inner"),
        P(("outer", "expert"), None, "inner"),
        P(("outer", "expert"), None, "inner"),
    )
    return jax.shard_map(
        local,
        mesh=mesh,
        in_specs=placed,
        out_specs=P(("parts", "outer", "expert"), "inner"),
        check_vma=False,
    )
```

```python
import functools

import jax
import jax.numpy as jnp
from jax import lax
from jax.experimental import pallas as pl
from jax.experimental.pallas import tpu as pltpu
from jax.sharding import PartitionSpec as P


CAP = 16
BATCHES = [[0, 3], [2, 1]]
SHARE_COST = 1e10
MIB = 1 << 20
VMEM = pl.BlockSpec(memory_space=pltpu.VMEM)
HBM = pl.BlockSpec(memory_space=pltpu.HBM)
BF16, F32 = jnp.bfloat16, jnp.float32


def call(body, outs, specs, cost, limit=16, out_space=VMEM, scratch=()):
    flops, moved = cost
    return pl.pallas_call(
        body,
        out_shape=[jax.ShapeDtypeStruct(s, d) for s, d in outs],
        in_specs=specs,
        out_specs=[out_space] * len(outs),
        scratch_shapes=scratch,
        compiler_params=pltpu.CompilerParams(vmem_limit_bytes=int(limit * MIB)),
        cost_estimate=pl.CostEstimate(flops=int(flops), bytes_accessed=moved, transcendentals=0),
    )


def turn(x, axis, by):
    size = lax.axis_size(axis)
    return lax.ppermute(x, axis, [(k, (k + by) % size) for k in range(size)])


def spread(order):
    steps = []
    for k in range(1, order):
        for step in (k, order - k):
            if step not in steps and 0 < step < order:
                steps.append(step)
    return steps


def experts():
    cores, depths = lax.axis_size("outer"), lax.axis_size("expert")
    core, depth = lax.axis_index("outer"), lax.axis_index("expert")
    return [
        lax.rem(core + c, cores) * depths + lax.rem(depth + s, depths)
        for c in range(cores)
        for s in range(depths)
    ]


def peer_part(p):
    peers = lax.axis_size("inner")
    return lax.rem(lax.axis_index("inner") + peers - p, peers)


def part_of(ref, p, depth):
    return ref[0, pl.ds(pl.multiple_of(peer_part(p) * depth, depth), depth), :]


def hits_of(order, ids):
    rows = [jnp.max(jnp.where(ids == e, 1.0, 0.0), axis=0, keepdims=True) for e in order]
    return jnp.concatenate(rows, axis=0)


def places(hits):
    groups, count = hits.shape
    before = lax.broadcasted_iota(jnp.int32, (count, count), 0)
    after = lax.broadcasted_iota(jnp.int32, (count, count), 1)
    earlier = jnp.dot(
        hits.astype(BF16),
        jnp.where(before < after, 1.0, 0.0).astype(BF16),
        preferred_element_type=F32,
    )
    slot = lax.broadcasted_iota(jnp.int32, (groups, CAP, count), 1).astype(F32)
    taken = jnp.where(hits > 0.5, earlier, -1.0)
    return jnp.where(taken[:, None, :] == slot, 1.0, 0.0)


def fill_kernel(parts, ids_hbm, tokens_hbm, *refs):
    outs, (ids_ref, tokens_ref, sems) = refs[: len(parts)], refs[len(parts) :]
    ids_copy = pltpu.make_async_copy(ids_hbm, ids_ref, sems.at[0])
    tokens_copy = pltpu.make_async_copy(tokens_hbm, tokens_ref, sems.at[1])
    ids_copy.start()
    tokens_copy.start()
    ids_copy.wait()
    order = experts()
    pick = places(hits_of(order, ids_ref[...]))
    pick = pick.reshape(len(order) * CAP, ids_ref.shape[1]).astype(BF16)
    tokens_copy.wait()
    rows = jnp.dot(pick, tokens_ref[...], preferred_element_type=F32).astype(BF16)
    at = 0
    for out, size in zip(outs, parts):
        out[...] = rows[at : at + size]
        at += size


def share_kernel(ids_hbm, num_hbm, high_ref, low_ref, ids_ref, num_ref, sems):
    ids_copy = pltpu.make_async_copy(ids_hbm, ids_ref, sems.at[0])
    num_copy = pltpu.make_async_copy(num_hbm, num_ref, sems.at[1])
    ids_copy.start()
    num_copy.start()
    ids_copy.wait()
    num_copy.wait()
    ids, order = ids_ref[...], experts()
    groups, count = len(order), ids.shape[1]
    num = num_ref[...].astype(F32)
    live = jnp.where(ids < groups, num, 0.0)
    total = jnp.maximum(jnp.sum(live, axis=0, keepdims=True), 1.0)
    given = [
        jnp.sum(jnp.where(ids == e, num, 0.0), axis=0, keepdims=True) / total for e in order
    ]
    weight = jnp.concatenate(given, axis=0)
    slots = places(hits_of(order, ids)) * weight[:, None, :]
    mix = slots.reshape(groups * CAP, count).T
    high = mix.astype(BF16)
    high_ref[...] = high
    low_ref[...] = (mix - high.astype(F32)).astype(BF16)


def rows_of(refs):
    return jnp.concatenate([r[...] for r in refs], axis=0)


def in_first_kernel(n, *refs):
    x, (gate_ref, up_ref, g_ref, u_ref) = rows_of(refs[:n]), refs[n:]
    depth = x.shape[1]
    g_ref[...] = jnp.dot(x, part_of(gate_ref, 0, depth), preferred_element_type=F32)
    u_ref[...] = jnp.dot(x, part_of(up_ref, 0, depth), preferred_element_type=F32)


def in_last_kernel(n, peers, *refs):
    xs, (gate_ref, up_ref, g_ref, u_ref, h_ref) = refs[: n * peers], refs[n * peers :]
    g, u = g_ref[...], u_ref[...]
    for p in range(peers):
        x = rows_of(xs[p * n : (p + 1) * n])
        depth = x.shape[1]
        g += jnp.dot(x, part_of(gate_ref, p + 1, depth), preferred_element_type=F32)
        u += jnp.dot(x, part_of(up_ref, p + 1, depth), preferred_element_type=F32)
    h_ref[...] = (g * jax.nn.sigmoid(g) * u).astype(BF16)


def out_first_kernel(h_ref, down_ref, o_ref):
    down = part_of(down_ref, 0, h_ref.shape[1])
    o_ref[...] = jnp.dot(h_ref[...], down, preferred_element_type=F32)


def out_last_kernel(peers, *refs):
    hs, (down_ref, o_ref), outs = refs[:peers], refs[peers : peers + 2], refs[peers + 2 :]
    total = o_ref[...]
    for p in range(peers):
        down = part_of(down_ref, p + 1, hs[p].shape[1])
        total += jnp.dot(hs[p][...], down, preferred_element_type=F32)
    size = outs[0].shape[0]
    for k, out in enumerate(outs):
        out[...] = total[k * size : (k + 1) * size].astype(BF16)


def mix_kernel(n, high_ref, low_ref, *refs):
    rows, (out_hbm, out_ref, sems) = rows_of(refs[:n]), refs[n:]
    width = out_ref.shape[1]
    block = min(512, width)
    copies = []
    for k in range(width // block):
        at = slice(k * block, (k + 1) * block)
        total = jnp.dot(high_ref[...], rows[:, at], preferred_element_type=F32)
        total += jnp.dot(low_ref[...], rows[:, at], preferred_element_type=F32)
        out_ref[:, at] = total.astype(BF16)
        copies.append(pltpu.make_async_copy(out_ref.at[:, at], out_hbm.at[:, at], sems.at[k]))
        copies[-1].start()
    for copy in copies:
        copy.wait()


def local(tokens, expert_ids, gate_num, gate_weight, up_weight, down_weight):
    cores, depths, peers = (lax.axis_size(a) for a in ("outer", "expert", "inner"))
    groups = cores * depths
    count, width = tokens.shape
    hidden_size = gate_weight.shape[2]
    out_width = down_weight.shape[2]
    slots = groups * CAP
    ids, num = expert_ids.T, gate_num.T
    steps = spread(depths)
    whole = depths > 4 or peers > 2
    batches = [[0] + steps] if whole else BATCHES

    parts = [CAP] * depths + [depths * CAP] * (cores - 1)
    sent = call(
        functools.partial(fill_kernel, parts),
        [((p, width), BF16) for p in parts],
        [HBM, HBM],
        (2 * slots * count * width, 4 * slots * width),
        53.2,
        scratch=[
            pltpu.VMEM(ids.shape, jnp.int32),
            pltpu.VMEM(tokens.shape, BF16),
            pltpu.SemaphoreType.DMA((2,)),
        ],
    )(ids, tokens)
    traded = [turn(sent[depths + c - 1], "outer", c) for c in range(1, cores)]
    chunks = [
        jnp.concatenate([sent[s]] + [t[s * CAP : (s + 1) * CAP] for t in traded], axis=0)
        for s in range(depths)
    ]
    here, there = {0: chunks[0]}, {}
    for s in steps:
        here[s] = turn(chunks[s], "expert", s)
    if whole:
        here = {0: jnp.concatenate([here[s] for s in batches[0]], axis=0)}
    for s, x in here.items():
        there[s] = [turn(x, "inner", p) for p in range(1, peers)]

    high, low = call(
        share_kernel,
        [((count, slots), BF16)] * 2,
        [HBM, HBM],
        (SHARE_COST, 4 * slots * count),
        scratch=[pltpu.VMEM(ids.shape, jnp.int32)] * 2 + [pltpu.SemaphoreType.DMA((2,))],
    )(ids, num)

    done = {}
    for batch in batches:
        held = [0] if whole else batch
        n, size = len(held), len(batch) * cores * CAP
        flops = 4 * size * width * hidden_size
        g, u = call(
            functools.partial(in_first_kernel, n),
            [((size, hidden_size), F32)] * 2,
            [VMEM] * (n + 2),
            (flops, 4 * width * hidden_size),
            28,
        )(*[here[s] for s in held], gate_weight, up_weight)
        (hidden,) = call(
            functools.partial(in_last_kernel, n, peers - 1),
            [((size, hidden_size), BF16)],
            [VMEM] * (n * (peers - 1) + 4),
            (flops * (peers - 1), 4 * width * hidden_size * (peers - 1)),
            28,
        )(*[there[s][p] for p in range(peers - 1) for s in held], gate_weight, up_weight, g, u)
        hidden_there = [turn(hidden, "inner", p) for p in range(1, peers)]
        flops = 2 * size * hidden_size * out_width
        (partial,) = call(
            out_first_kernel,
            [((size, out_width), F32)],
            [VMEM, VMEM],
            (flops, 2 * hidden_size * out_width),
            20,
        )(hidden, down_weight)
        outs = call(
            functools.partial(out_last_kernel, peers - 1),
            [((cores * CAP, out_width), BF16)] * len(batch),
            [VMEM] * (peers + 1),
            (flops * (peers - 1), 2 * hidden_size * out_width * (peers - 1)),
            20,
        )(*hidden_there, down_weight, partial)
        done.update(zip(batch, outs))

    back = {0: done[0]}
    for s in steps:
        back[s] = turn(done[s], "expert", depths - s)
    final = [back[s][:CAP] for s in range(depths)]
    for c in range(1, cores):
        for s in range(depths):
            final.append(turn(back[s][c * CAP : (c + 1) * CAP], "outer", cores - c))
    (mixed,) = call(
        functools.partial(mix_kernel, len(final)),
        [((count, out_width), BF16)],
        [VMEM] * (2 + len(final)),
        (4 * count * slots * out_width, 4 * count * out_width),
        out_space=HBM,
        scratch=[
            pltpu.VMEM((count, out_width), BF16),
            pltpu.SemaphoreType.DMA((max(1, out_width // 512),)),
        ],
    )(high, low, *final)
    return mixed


def solution(mesh):
    placed = (
        P(("parts", "outer", "expert"), "inner"),
        P(("parts", "outer", "expert"), None),
        P(("parts", "outer", "expert"), None),
        P(("outer", "expert"), None, "inner"),
        P(("outer", "expert"), None, "inner"),
        P(("outer", "expert"), None, "inner"),
    )

    return jax.shard_map(
        local,
        mesh=mesh,
        in_specs=placed,
        out_specs=P(("parts", "outer", "expert"), "inner"),
        check_vma=False,
    )
```

```python
import functools

import jax
import jax.numpy as jnp
from jax import lax
from jax.experimental import pallas as pl
from jax.experimental.pallas import tpu as pltpu
from jax.sharding import PartitionSpec as P


CAP = 16
BATCHES = [[0, 3], [2, 1]]
SHARE_COST = 1e10
LOAD_COST = 3e9
LATE, EARLY = [3], []
MIB = 1 << 20
VMEM = pl.BlockSpec(memory_space=pltpu.VMEM)
HBM = pl.BlockSpec(memory_space=pltpu.HBM)
BF16, F32 = jnp.bfloat16, jnp.float32


def call(body, outs, specs, cost, limit=16, out_space=VMEM, scratch=()):
    flops, moved = cost
    return pl.pallas_call(
        body,
        out_shape=[jax.ShapeDtypeStruct(s, d) for s, d in outs],
        in_specs=specs,
        out_specs=[out_space] * len(outs),
        scratch_shapes=scratch,
        compiler_params=pltpu.CompilerParams(vmem_limit_bytes=int(limit * MIB)),
        cost_estimate=pl.CostEstimate(flops=int(flops), bytes_accessed=moved, transcendentals=0),
    )


def turn(x, axis, by):
    size = lax.axis_size(axis)
    return lax.ppermute(x, axis, [(k, (k + by) % size) for k in range(size)])


def exchange(chunk, cores, way):
    blocks = [chunk[:CAP]]
    for c in range(1, cores):
        blocks.append(turn(chunk[c * CAP : (c + 1) * CAP], "outer", (way * c) % cores))
    return jnp.concatenate(blocks, axis=0)


def spread(order):
    steps = []
    for k in range(1, order):
        for step in (k, order - k):
            if step not in steps and 0 < step < order:
                steps.append(step)
    return steps


def experts(pairs):
    cores, depths = lax.axis_size("outer"), lax.axis_size("expert")
    core, depth = lax.axis_index("outer"), lax.axis_index("expert")
    return [lax.rem(core + c, cores) * depths + lax.rem(depth + s, depths) for c, s in pairs]


def peer_part(p):
    peers = lax.axis_size("inner")
    return lax.rem(lax.axis_index("inner") + peers - p, peers)


def part_of(ref, p, depth, at):
    return ref[0, pl.ds(pl.multiple_of(peer_part(p) * depth, depth), depth), at]


def hits_of(order, ids):
    rows = [jnp.max(jnp.where(ids == e, 1.0, 0.0), axis=0, keepdims=True) for e in order]
    return jnp.concatenate(rows, axis=0)


def places(hits):
    groups, count = hits.shape
    before = lax.broadcasted_iota(jnp.int32, (count, count), 0)
    after = lax.broadcasted_iota(jnp.int32, (count, count), 1)
    earlier = jnp.dot(
        hits.astype(BF16),
        jnp.where(before < after, 1.0, 0.0).astype(BF16),
        preferred_element_type=F32,
    )
    slot = lax.broadcasted_iota(jnp.int32, (groups, CAP, count), 1).astype(F32)
    taken = jnp.where(hits > 0.5, earlier, -1.0)
    return jnp.where(taken[:, None, :] == slot, 1.0, 0.0)


def blocks_of(width, size=256):
    return [slice(at, min(at + size, width)) for at in range(0, width, size)]


def load_kernel(pieces, from_hbm, to_ref, sems):
    size = from_hbm.shape[0] // pieces
    copies = []
    for k in range(pieces):
        at = slice(k * size, (k + 1) * size)
        copies.append(pltpu.make_async_copy(from_hbm.at[at], to_ref.at[at], sems.at[k]))
        copies[-1].start()
    for copy in copies:
        copy.wait()


def fill_kernel(pairs, parts, ids_ref, tokens_ref, *outs):
    order = experts(pairs)
    pick = places(hits_of(order, ids_ref[...]))
    pick = pick.reshape(len(order) * CAP, ids_ref.shape[1]).astype(BF16)
    for at in blocks_of(tokens_ref.shape[1]):
        rows = jnp.dot(pick, tokens_ref[:, at], preferred_element_type=F32).astype(BF16)
        row = 0
        for out, size in zip(outs, parts):
            out[:, at] = rows[row : row + size]
            row += size


def share_kernel(pairs, ids_hbm, num_hbm, high_ref, low_ref, ids_ref, num_ref, sems):
    ids_copy = pltpu.make_async_copy(ids_hbm, ids_ref, sems.at[0])
    num_copy = pltpu.make_async_copy(num_hbm, num_ref, sems.at[1])
    ids_copy.start()
    num_copy.start()
    ids_copy.wait()
    num_copy.wait()
    ids, order = ids_ref[...], experts(pairs)
    groups, count = len(order), ids.shape[1]
    num = num_ref[...].astype(F32)
    live = jnp.where(ids < groups, num, 0.0)
    total = jnp.maximum(jnp.sum(live, axis=0, keepdims=True), 1.0)
    given = [
        jnp.sum(jnp.where(ids == e, num, 0.0), axis=0, keepdims=True) / total for e in order
    ]
    weight = jnp.concatenate(given, axis=0)
    slots = places(hits_of(order, ids)) * weight[:, None, :]
    mix = slots.reshape(groups * CAP, count).T
    high = mix.astype(BF16)
    high_ref[...] = high
    low_ref[...] = (mix - high.astype(F32)).astype(BF16)


def rows_of(refs, at=slice(None)):
    return jnp.concatenate([r[:, at] for r in refs], axis=0)


def filled(x):
    return x if x.shape[0] >= 128 else jnp.concatenate([x, x], axis=0)


def in_first_kernel(n, *refs):
    x, (gate_ref, up_ref, g_ref, u_ref) = rows_of(refs[:n]), refs[n:]
    size, depth = x.shape
    x = filled(x)
    for at in blocks_of(g_ref.shape[1]):
        g_ref[:, at] = jnp.dot(x, part_of(gate_ref, 0, depth, at), preferred_element_type=F32)[:size]
        u_ref[:, at] = jnp.dot(x, part_of(up_ref, 0, depth, at), preferred_element_type=F32)[:size]


def in_last_kernel(n, peers, *refs):
    xs, (gate_ref, up_ref, g_ref, u_ref, h_ref) = refs[: n * peers], refs[n * peers :]
    xs = [rows_of(xs[p * n : (p + 1) * n]) for p in range(peers)]
    size = xs[0].shape[0]
    xs = [filled(x) for x in xs]
    for at in blocks_of(h_ref.shape[1]):
        g, u = g_ref[:, at], u_ref[:, at]
        for p, x in enumerate(xs):
            depth = x.shape[1]
            g += jnp.dot(x, part_of(gate_ref, p + 1, depth, at), preferred_element_type=F32)[:size]
            u += jnp.dot(x, part_of(up_ref, p + 1, depth, at), preferred_element_type=F32)[:size]
        h_ref[:, at] = (g * jax.nn.sigmoid(g) * u).astype(BF16)


def out_first_kernel(h_ref, down_ref, o_ref):
    h = h_ref[...]
    for at in blocks_of(o_ref.shape[1]):
        down = part_of(down_ref, 0, h.shape[1], at)
        o_ref[:, at] = jnp.dot(h, down, preferred_element_type=F32)


def out_last_kernel(peers, *refs):
    hs, (down_ref, o_ref), outs = refs[:peers], refs[peers : peers + 2], refs[peers + 2 :]
    size = outs[0].shape[0]
    for at in blocks_of(o_ref.shape[1]):
        total = o_ref[:, at]
        for p in range(peers):
            down = part_of(down_ref, p + 1, hs[p].shape[1], at)
            total += jnp.dot(hs[p][...], down, preferred_element_type=F32)
        for k, out in enumerate(outs):
            out[:, at] = total[k * size : (k + 1) * size].astype(BF16)


def mix_kernel(n, high_ref, low_ref, *refs):
    rows, (out_hbm, out_ref, sems) = refs[:n], refs[n:]
    high, low = high_ref[...], low_ref[...]
    copies = []
    for k, at in enumerate(blocks_of(out_ref.shape[1])):
        x = rows_of(rows, at)
        total = jnp.dot(high, x, preferred_element_type=F32)
        total += jnp.dot(low, x, preferred_element_type=F32)
        out_ref[:, at] = total.astype(BF16)
        copies.append(pltpu.make_async_copy(out_ref.at[:, at], out_hbm.at[:, at], sems.at[k]))
        copies[-1].start()
    for copy in copies:
        copy.wait()


def local(tokens, expert_ids, gate_num, gate_weight, up_weight, down_weight):
    cores, depths, peers = (lax.axis_size(a) for a in ("outer", "expert", "inner"))
    groups = cores * depths
    count, width = tokens.shape
    hidden_size = gate_weight.shape[2]
    out_width = down_weight.shape[2]
    slots = groups * CAP
    ids, num = expert_ids.T, gate_num.T
    steps = spread(depths)
    whole = depths > 4 or peers > 2
    batches = [[0] + steps] if whole else BATCHES
    late, early = ([], []) if whole else (LATE, EARLY)
    soon = [s for s in range(depths) if s not in late]

    pairs = [(c, s) for s in late for c in range(cores)]
    pairs += [(c, s) for c in range(cores) for s in soon]
    parts = [cores * CAP] * len(late) + [CAP] * len(soon) + [len(soon) * CAP] * (cores - 1)
    (tokens,) = call(
        functools.partial(load_kernel, 4),
        [(tokens.shape, BF16)],
        [HBM],
        (LOAD_COST, 2 * tokens.size),
        53.2,
        scratch=[pltpu.SemaphoreType.DMA((4,))],
    )(tokens)
    sent = call(
        functools.partial(fill_kernel, pairs, parts),
        [((p, width), BF16) for p in parts],
        [VMEM, VMEM],
        (2 * slots * count * width, 4 * slots * width),
    )(ids, tokens)
    traded = [turn(x, "outer", c + 1) for c, x in enumerate(sent[len(late) + len(soon) :])]
    chunks = dict(zip(late, sent))
    for k, s in enumerate(soon):
        blocks = [sent[len(late) + k]] + [t[k * CAP : (k + 1) * CAP] for t in traded]
        chunks[s] = jnp.concatenate(blocks, axis=0)
    here, there = {0: chunks[0]}, {}
    for s in steps:
        here[s] = turn(chunks[s], "expert", s)
        if s in late:
            here[s] = exchange(here[s], cores, 1)
    if whole:
        here = {0: jnp.concatenate([here[s] for s in batches[0]], axis=0)}
    for s, x in here.items():
        there[s] = [turn(x, "inner", p) for p in range(1, peers)]

    done = {}
    for batch in batches:
        held = [0] if whole else batch
        n, size = len(held), len(batch) * cores * CAP
        flops = 4 * size * width * hidden_size
        g, u = call(
            functools.partial(in_first_kernel, n),
            [((size, hidden_size), F32)] * 2,
            [VMEM] * (n + 2),
            (flops, 4 * width * hidden_size),
            28,
        )(*[here[s] for s in held], gate_weight, up_weight)
        (hidden,) = call(
            functools.partial(in_last_kernel, n, peers - 1),
            [((size, hidden_size), BF16)],
            [VMEM] * (n * (peers - 1) + 4),
            (flops * (peers - 1), 4 * width * hidden_size * (peers - 1)),
            28,
        )(*[there[s][p] for p in range(peers - 1) for s in held], gate_weight, up_weight, g, u)
        hidden_there = [turn(hidden, "inner", p) for p in range(1, peers)]
        flops = 2 * size * hidden_size * out_width
        (partial,) = call(
            out_first_kernel,
            [((size, out_width), F32)],
            [VMEM, VMEM],
            (flops, 2 * hidden_size * out_width),
            20,
        )(hidden, down_weight)
        outs = call(
            functools.partial(out_last_kernel, peers - 1),
            [((cores * CAP, out_width), BF16)] * len(batch),
            [VMEM] * (peers + 1),
            (flops * (peers - 1), 2 * hidden_size * out_width * (peers - 1)),
            20,
        )(*hidden_there, down_weight, partial)
        done.update(zip(batch, outs))

    final, pairs = [], []
    for s in [0] + steps:
        x = done[s]
        if s in early:
            x = exchange(x, cores, -1)
        if s:
            x = turn(x, "expert", depths - s)
        if s not in early:
            x = exchange(x, cores, -1)
        final.append(x)
        pairs += [(c, s) for c in range(cores)]

    high, low = call(
        functools.partial(share_kernel, pairs),
        [((count, slots), BF16)] * 2,
        [HBM, HBM],
        (SHARE_COST, 4 * slots * count),
        scratch=[pltpu.VMEM(ids.shape, jnp.int32)] * 2 + [pltpu.SemaphoreType.DMA((2,))],
    )(ids, num)
    (mixed,) = call(
        functools.partial(mix_kernel, len(final)),
        [((count, out_width), BF16)],
        [VMEM] * (2 + len(final)),
        (4 * count * slots * out_width, 4 * count * out_width),
        out_space=HBM,
        scratch=[
            pltpu.VMEM((count, out_width), BF16),
            pltpu.SemaphoreType.DMA((len(blocks_of(out_width)),)),
        ],
    )(high, low, *final)
    return mixed


def solution(mesh):
    placed = (
        P(("parts", "outer", "expert"), "inner"),
        P(("parts", "outer", "expert"), None),
        P(("parts", "outer", "expert"), None),
        P(("outer", "expert"), None, "inner"),
        P(("outer", "expert"), None, "inner"),
        P(("outer", "expert"), None, "inner"),
    )

    return jax.shard_map(
        local,
        mesh=mesh,
        in_specs=placed,
        out_specs=P(("parts", "outer", "expert"), "inner"),
        check_vma=False,
    )
```

```python
import functools

import jax
import jax.numpy as jnp
from jax import lax
from jax.experimental import pallas as pl
from jax.experimental.pallas import tpu as pltpu
from jax.sharding import PartitionSpec as P


CAP = 16
BATCHES = [[0, 3], [2, 1]]
SHARE_COST = 1e10
LOAD_COST = 3e9
LATE, WIDE, DIRECT = [3], [1], [2, 1]
MIB = 1 << 20
VMEM = pl.BlockSpec(memory_space=pltpu.VMEM)
HBM = pl.BlockSpec(memory_space=pltpu.HBM)
BF16, F32 = jnp.bfloat16, jnp.float32


def call(body, outs, specs, cost, limit=16, out_space=VMEM, scratch=()):
    flops, moved = cost
    return pl.pallas_call(
        body,
        out_shape=[jax.ShapeDtypeStruct(s, d) for s, d in outs],
        in_specs=specs,
        out_specs=[out_space] * len(outs),
        scratch_shapes=scratch,
        compiler_params=pltpu.CompilerParams(vmem_limit_bytes=int(limit * MIB)),
        cost_estimate=pl.CostEstimate(flops=int(flops), bytes_accessed=moved, transcendentals=0),
    )


def turn(x, axis, by):
    size = lax.axis_size(axis)
    return lax.ppermute(x, axis, [(k, (k + by) % size) for k in range(size)])


def turn_both(x, up, along):
    cores, depths = lax.axis_size("outer"), lax.axis_size("expert")
    pairs = [
        (o * depths + z, (o + up) % cores * depths + (z + along) % depths)
        for o in range(cores)
        for z in range(depths)
    ]
    return lax.ppermute(x, ("outer", "expert"), pairs)


def exchange(chunk, cores, way):
    blocks = [chunk[:CAP]]
    for c in range(1, cores):
        blocks.append(turn(chunk[c * CAP : (c + 1) * CAP], "outer", (way * c) % cores))
    return jnp.concatenate(blocks, axis=0)


def spread(order):
    steps = []
    for k in range(1, order):
        for step in (k, order - k):
            if step not in steps and 0 < step < order:
                steps.append(step)
    return steps


def experts(pairs):
    cores, depths = lax.axis_size("outer"), lax.axis_size("expert")
    core, depth = lax.axis_index("outer"), lax.axis_index("expert")
    return [lax.rem(core + c, cores) * depths + lax.rem(depth + s, depths) for c, s in pairs]


def peer_part(p):
    peers = lax.axis_size("inner")
    return lax.rem(lax.axis_index("inner") + peers - p, peers)


def part_of(ref, p, depth, at):
    return ref[0, pl.ds(pl.multiple_of(peer_part(p) * depth, depth), depth), at]


def hits_of(order, ids):
    rows = [jnp.max(jnp.where(ids == e, 1.0, 0.0), axis=0, keepdims=True) for e in order]
    return jnp.concatenate(rows, axis=0)


def places(hits):
    groups, count = hits.shape
    before = lax.broadcasted_iota(jnp.int32, (count, count), 0)
    after = lax.broadcasted_iota(jnp.int32, (count, count), 1)
    earlier = jnp.dot(
        hits.astype(BF16),
        jnp.where(before < after, 1.0, 0.0).astype(BF16),
        preferred_element_type=F32,
    )
    slot = lax.broadcasted_iota(jnp.int32, (groups, CAP, count), 1).astype(F32)
    taken = jnp.where(hits > 0.5, earlier, -1.0)
    return jnp.where(taken[:, None, :] == slot, 1.0, 0.0)


def blocks_of(width, size=256):
    return [slice(at, min(at + size, width)) for at in range(0, width, size)]


def load_kernel(pieces, from_hbm, to_ref, sems):
    size = from_hbm.shape[0] // pieces
    copies = []
    for k in range(pieces):
        at = slice(k * size, (k + 1) * size)
        copies.append(pltpu.make_async_copy(from_hbm.at[at], to_ref.at[at], sems.at[k]))
        copies[-1].start()
    for copy in copies:
        copy.wait()


def fill_kernel(pairs, parts, ids_ref, tokens_ref, *outs):
    order = experts(pairs)
    pick = places(hits_of(order, ids_ref[...]))
    pick = pick.reshape(len(order) * CAP, ids_ref.shape[1]).astype(BF16)
    for at in blocks_of(tokens_ref.shape[1]):
        rows = jnp.dot(pick, tokens_ref[:, at], preferred_element_type=F32).astype(BF16)
        row = 0
        for out, size in zip(outs, parts):
            out[:, at] = rows[row : row + size]
            row += size


def share_kernel(pairs, ids_hbm, num_hbm, high_ref, low_ref, ids_ref, num_ref, sems):
    ids_copy = pltpu.make_async_copy(ids_hbm, ids_ref, sems.at[0])
    num_copy = pltpu.make_async_copy(num_hbm, num_ref, sems.at[1])
    ids_copy.start()
    num_copy.start()
    ids_copy.wait()
    num_copy.wait()
    ids, order = ids_ref[...], experts(pairs)
    groups, count = len(order), ids.shape[1]
    num = num_ref[...].astype(F32)
    live = jnp.where(ids < groups, num, 0.0)
    total = jnp.maximum(jnp.sum(live, axis=0, keepdims=True), 1.0)
    given = [
        jnp.sum(jnp.where(ids == e, num, 0.0), axis=0, keepdims=True) / total for e in order
    ]
    weight = jnp.concatenate(given, axis=0)
    slots = places(hits_of(order, ids)) * weight[:, None, :]
    mix = slots.reshape(groups * CAP, count).T
    high = mix.astype(BF16)
    high_ref[...] = high
    low_ref[...] = (mix - high.astype(F32)).astype(BF16)


def rows_of(refs, at=slice(None)):
    return jnp.concatenate([r[:, at] for r in refs], axis=0)


def filled(x):
    return x if x.shape[0] >= 128 else jnp.concatenate([x, x], axis=0)


def in_first_kernel(n, *refs):
    x, (gate_ref, up_ref, g_ref, u_ref) = rows_of(refs[:n]), refs[n:]
    size, depth = x.shape
    x = filled(x)
    for at in blocks_of(g_ref.shape[1]):
        g_ref[:, at] = jnp.dot(x, part_of(gate_ref, 0, depth, at), preferred_element_type=F32)[:size]
        u_ref[:, at] = jnp.dot(x, part_of(up_ref, 0, depth, at), preferred_element_type=F32)[:size]


def in_last_kernel(n, peers, *refs):
    xs, (gate_ref, up_ref, g_ref, u_ref, h_ref) = refs[: n * peers], refs[n * peers :]
    xs = [rows_of(xs[p * n : (p + 1) * n]) for p in range(peers)]
    size = xs[0].shape[0]
    xs = [filled(x) for x in xs]
    for at in blocks_of(h_ref.shape[1]):
        g, u = g_ref[:, at], u_ref[:, at]
        for p, x in enumerate(xs):
            depth = x.shape[1]
            g += jnp.dot(x, part_of(gate_ref, p + 1, depth, at), preferred_element_type=F32)[:size]
            u += jnp.dot(x, part_of(up_ref, p + 1, depth, at), preferred_element_type=F32)[:size]
        h_ref[:, at] = (g * jax.nn.sigmoid(g) * u).astype(BF16)


def out_first_kernel(h_ref, down_ref, o_ref):
    h = h_ref[...]
    for at in blocks_of(o_ref.shape[1]):
        down = part_of(down_ref, 0, h.shape[1], at)
        o_ref[:, at] = jnp.dot(h, down, preferred_element_type=F32)


def out_last_kernel(peers, *refs):
    hs, (down_ref, o_ref), outs = refs[:peers], refs[peers : peers + 2], refs[peers + 2 :]
    for at in blocks_of(o_ref.shape[1]):
        total = o_ref[:, at]
        for p in range(peers):
            down = part_of(down_ref, p + 1, hs[p].shape[1], at)
            total += jnp.dot(hs[p][...], down, preferred_element_type=F32)
        row = 0
        for out in outs:
            out[:, at] = total[row : row + out.shape[0]].astype(BF16)
            row += out.shape[0]


def mix_kernel(n, high_ref, low_ref, *refs):
    rows, (out_hbm, out_ref, sems) = refs[:n], refs[n:]
    high, low = high_ref[...], low_ref[...]
    copies = []
    for k, at in enumerate(blocks_of(out_ref.shape[1])):
        x = rows_of(rows, at)
        total = jnp.dot(high, x, preferred_element_type=F32)
        total += jnp.dot(low, x, preferred_element_type=F32)
        out_ref[:, at] = total.astype(BF16)
        copies.append(pltpu.make_async_copy(out_ref.at[:, at], out_hbm.at[:, at], sems.at[k]))
        copies[-1].start()
    for copy in copies:
        copy.wait()


def local(tokens, expert_ids, gate_num, gate_weight, up_weight, down_weight):
    cores, depths, peers = (lax.axis_size(a) for a in ("outer", "expert", "inner"))
    groups = cores * depths
    count, width = tokens.shape
    hidden_size = gate_weight.shape[2]
    out_width = down_weight.shape[2]
    slots = groups * CAP
    ids, num = expert_ids.T, gate_num.T
    steps = spread(depths)
    whole = depths > 4 or peers > 2
    batches = [[0] + steps] if whole else BATCHES
    late, wide, direct = ([], [], []) if whole else (LATE, WIDE, DIRECT)
    soon = [s for s in range(depths) if s not in late]

    pairs = [(c, s) for s in late for c in range(cores)]
    pairs += [(c, s) for c in range(cores) for s in soon]
    parts = [cores * CAP] * len(late) + [CAP] * len(soon) + [len(soon) * CAP] * (cores - 1)
    (tokens,) = call(
        functools.partial(load_kernel, 4),
        [(tokens.shape, BF16)],
        [HBM],
        (LOAD_COST, 2 * tokens.size),
        53.2,
        scratch=[pltpu.SemaphoreType.DMA((4,))],
    )(tokens)
    sent = call(
        functools.partial(fill_kernel, pairs, parts),
        [((p, width), BF16) for p in parts],
        [VMEM, VMEM],
        (2 * slots * count * width, 4 * slots * width),
    )(ids, tokens)
    traded = [turn(x, "outer", c + 1) for c, x in enumerate(sent[len(late) + len(soon) :])]
    chunks = dict(zip(late, sent))
    for k, s in enumerate(soon):
        blocks = [sent[len(late) + k]] + [t[k * CAP : (k + 1) * CAP] for t in traded]
        chunks[s] = jnp.concatenate(blocks, axis=0)
    here, there = {0: chunks[0]}, {}
    for s in steps:
        here[s] = turn(chunks[s], "expert", s)
        if s in late:
            here[s] = exchange(here[s], cores, 1)
        if s in wide:
            there[s] = [turn(chunks[s], "inner", p) for p in range(1, peers)]
            there[s] = [turn(x, "expert", s) for x in there[s]]
    if whole:
        here = {0: jnp.concatenate([here[s] for s in batches[0]], axis=0)}
    for s, x in here.items():
        if s not in wide:
            there[s] = [turn(x, "inner", p) for p in range(1, peers)]

    done = {}
    for batch in batches:
        held = [0] if whole else batch
        n, size = len(held), len(batch) * cores * CAP
        flops = 4 * size * width * hidden_size
        g, u = call(
            functools.partial(in_first_kernel, n),
            [((size, hidden_size), F32)] * 2,
            [VMEM] * (n + 2),
            (flops, 4 * width * hidden_size),
            28,
        )(*[here[s] for s in held], gate_weight, up_weight)
        (hidden,) = call(
            functools.partial(in_last_kernel, n, peers - 1),
            [((size, hidden_size), BF16)],
            [VMEM] * (n * (peers - 1) + 4),
            (flops * (peers - 1), 4 * width * hidden_size * (peers - 1)),
            28,
        )(*[there[s][p] for p in range(peers - 1) for s in held], gate_weight, up_weight, g, u)
        hidden_there = [turn(hidden, "inner", p) for p in range(1, peers)]
        flops = 2 * size * hidden_size * out_width
        (partial,) = call(
            out_first_kernel,
            [((size, out_width), F32)],
            [VMEM, VMEM],
            (flops, 2 * hidden_size * out_width),
            20,
        )(hidden, down_weight)
        outs = list(call(
            functools.partial(out_last_kernel, peers - 1),
            [
                ((size, out_width), BF16)
                for s in batch
                for size in ([CAP] * cores if s in direct else [cores * CAP])
            ],
            [VMEM] * (peers + 1),
            (flops * (peers - 1), 2 * hidden_size * out_width * (peers - 1)),
            20,
        )(*hidden_there, down_weight, partial))
        for s in batch:
            done[s] = [outs.pop(0) for _ in range(cores if s in direct else 1)]

    final, pairs = [], []
    for s in [0] + steps:
        if s in direct:
            for c in range(cores):
                final.append(turn_both(done[s][c], -c, -s))
        else:
            (x,) = done[s]
            if s:
                x = turn(x, "expert", depths - s)
            final.append(exchange(x, cores, -1))
        pairs += [(c, s) for c in range(cores)]

    high, low = call(
        functools.partial(share_kernel, pairs),
        [((count, slots), BF16)] * 2,
        [HBM, HBM],
        (SHARE_COST, 4 * slots * count),
        scratch=[pltpu.VMEM(ids.shape, jnp.int32)] * 2 + [pltpu.SemaphoreType.DMA((2,))],
    )(ids, num)
    (mixed,) = call(
        functools.partial(mix_kernel, len(final)),
        [((count, out_width), BF16)],
        [VMEM] * (2 + len(final)),
        (4 * count * slots * out_width, 4 * count * out_width),
        out_space=HBM,
        scratch=[
            pltpu.VMEM((count, out_width), BF16),
            pltpu.SemaphoreType.DMA((len(blocks_of(out_width)),)),
        ],
    )(high, low, *final)
    return mixed


def solution(mesh):
    placed = (
        P(("parts", "outer", "expert"), "inner"),
        P(("parts", "outer", "expert"), None),
        P(("parts", "outer", "expert"), None),
        P(("outer", "expert"), None, "inner"),
        P(("outer", "expert"), None, "inner"),
        P(("outer", "expert"), None, "inner"),
    )

    return jax.shard_map(
        local,
        mesh=mesh,
        in_specs=placed,
        out_specs=P(("parts", "outer", "expert"), "inner"),
        check_vma=False,
    )
```

```python
import functools

import jax
import jax.numpy as jnp
from jax import lax
from jax.experimental import pallas as pl
from jax.experimental.pallas import tpu as pltpu
from jax.sharding import PartitionSpec as P


CAP = 16
PLANNED = (2, 4, 2)
BATCHES = [[0, 3], [2, 1]]
SHARE_COST = 1e10
LOAD_COST = 3e9
LATE, WIDE, DIRECT = [3], [1], [2, 1]
MIB = 1 << 20
VMEM = pl.BlockSpec(memory_space=pltpu.VMEM)
HBM = pl.BlockSpec(memory_space=pltpu.HBM)
BF16, F32 = jnp.bfloat16, jnp.float32


def call(body, outs, specs, cost, limit=16, out_space=VMEM, scratch=()):
    flops, moved = cost
    return pl.pallas_call(
        body,
        out_shape=[jax.ShapeDtypeStruct(s, d) for s, d in outs],
        in_specs=specs,
        out_specs=[out_space] * len(outs),
        scratch_shapes=scratch,
        compiler_params=pltpu.CompilerParams(vmem_limit_bytes=int(limit * MIB)),
        cost_estimate=pl.CostEstimate(flops=int(flops), bytes_accessed=moved, transcendentals=0),
    )


def turn(x, axis, by):
    size = lax.axis_size(axis)
    return lax.ppermute(x, axis, [(k, (k + by) % size) for k in range(size)])


def turn_both(x, up, along):
    cores, depths = lax.axis_size("outer"), lax.axis_size("expert")
    pairs = [
        (o * depths + z, (o + up) % cores * depths + (z + along) % depths)
        for o in range(cores)
        for z in range(depths)
    ]
    return lax.ppermute(x, ("outer", "expert"), pairs)


def exchange(chunk, cores, way):
    blocks = [chunk[:CAP]]
    for c in range(1, cores):
        blocks.append(turn(chunk[c * CAP : (c + 1) * CAP], "outer", (way * c) % cores))
    return jnp.concatenate(blocks, axis=0)


def spread(order):
    steps = []
    for k in range(1, order):
        for step in (k, order - k):
            if step not in steps and 0 < step < order:
                steps.append(step)
    return steps


def experts(pairs):
    cores, depths = lax.axis_size("outer"), lax.axis_size("expert")
    core, depth = lax.axis_index("outer"), lax.axis_index("expert")
    return [lax.rem(core + c, cores) * depths + lax.rem(depth + s, depths) for c, s in pairs]


def peer_part(p):
    peers = lax.axis_size("inner")
    return lax.rem(lax.axis_index("inner") + peers - p, peers)


def part_of(ref, p, depth, at):
    return ref[0, pl.ds(pl.multiple_of(peer_part(p) * depth, depth), depth), at]


def hits_of(order, ids):
    rows = [jnp.max(jnp.where(ids == e, 1.0, 0.0), axis=0, keepdims=True) for e in order]
    return jnp.concatenate(rows, axis=0)


def places(hits):
    groups, count = hits.shape
    before = lax.broadcasted_iota(jnp.int32, (count, count), 0)
    after = lax.broadcasted_iota(jnp.int32, (count, count), 1)
    earlier = jnp.dot(
        hits.astype(BF16),
        jnp.where(before < after, 1.0, 0.0).astype(BF16),
        preferred_element_type=F32,
    )
    slot = lax.broadcasted_iota(jnp.int32, (groups, CAP, count), 1).astype(F32)
    taken = jnp.where(hits > 0.5, earlier, -1.0)
    return jnp.where(taken[:, None, :] == slot, 1.0, 0.0)


def blocks_of(width, size=256):
    return [slice(at, min(at + size, width)) for at in range(0, width, size)]


def load_kernel(pieces, from_hbm, to_ref, sems):
    size = from_hbm.shape[0] // pieces
    copies = []
    for k in range(pieces):
        at = slice(k * size, (k + 1) * size)
        copies.append(pltpu.make_async_copy(from_hbm.at[at], to_ref.at[at], sems.at[k]))
        copies[-1].start()
    for copy in copies:
        copy.wait()


def fill_kernel(pairs, parts, ids_ref, tokens_ref, *outs):
    order = experts(pairs)
    pick = places(hits_of(order, ids_ref[...]))
    pick = pick.reshape(len(order) * CAP, ids_ref.shape[1]).astype(BF16)
    for at in blocks_of(tokens_ref.shape[1]):
        rows = jnp.dot(pick, tokens_ref[:, at], preferred_element_type=F32).astype(BF16)
        row = 0
        for out, size in zip(outs, parts):
            out[:, at] = rows[row : row + size]
            row += size


def share_kernel(pairs, ids_hbm, num_hbm, high_ref, low_ref, ids_ref, num_ref, sems):
    ids_copy = pltpu.make_async_copy(ids_hbm, ids_ref, sems.at[0])
    num_copy = pltpu.make_async_copy(num_hbm, num_ref, sems.at[1])
    ids_copy.start()
    num_copy.start()
    ids_copy.wait()
    num_copy.wait()
    ids, order = ids_ref[...], experts(pairs)
    groups, count = len(order), ids.shape[1]
    num = num_ref[...].astype(F32)
    live = jnp.where(ids < groups, num, 0.0)
    total = jnp.maximum(jnp.sum(live, axis=0, keepdims=True), 1.0)
    given = [
        jnp.sum(jnp.where(ids == e, num, 0.0), axis=0, keepdims=True) / total for e in order
    ]
    weight = jnp.concatenate(given, axis=0)
    slots = places(hits_of(order, ids)) * weight[:, None, :]
    mix = slots.reshape(groups * CAP, count).T
    high = mix.astype(BF16)
    high_ref[...] = high
    low_ref[...] = (mix - high.astype(F32)).astype(BF16)


def rows_of(refs, at=slice(None)):
    return jnp.concatenate([r[:, at] for r in refs], axis=0)


def filled(x):
    return x if x.shape[0] >= 128 else jnp.concatenate([x, x], axis=0)


def in_first_kernel(n, *refs):
    x, (gate_ref, up_ref, g_ref, u_ref) = rows_of(refs[:n]), refs[n:]
    size, depth = x.shape
    x = filled(x)
    for at in blocks_of(g_ref.shape[1]):
        g_ref[:, at] = jnp.dot(x, part_of(gate_ref, 0, depth, at), preferred_element_type=F32)[:size]
        u_ref[:, at] = jnp.dot(x, part_of(up_ref, 0, depth, at), preferred_element_type=F32)[:size]


def in_last_kernel(n, peers, *refs):
    xs, (gate_ref, up_ref, g_ref, u_ref, h_ref) = refs[: n * peers], refs[n * peers :]
    xs = [rows_of(xs[p * n : (p + 1) * n]) for p in range(peers)]
    size = xs[0].shape[0]
    xs = [filled(x) for x in xs]
    for at in blocks_of(h_ref.shape[1]):
        g, u = g_ref[:, at], u_ref[:, at]
        for p, x in enumerate(xs):
            depth = x.shape[1]
            g += jnp.dot(x, part_of(gate_ref, p + 1, depth, at), preferred_element_type=F32)[:size]
            u += jnp.dot(x, part_of(up_ref, p + 1, depth, at), preferred_element_type=F32)[:size]
        h_ref[:, at] = (g * jax.nn.sigmoid(g) * u).astype(BF16)


def out_first_kernel(h_ref, down_ref, o_ref):
    h = h_ref[...]
    for at in blocks_of(o_ref.shape[1]):
        down = part_of(down_ref, 0, h.shape[1], at)
        o_ref[:, at] = jnp.dot(h, down, preferred_element_type=F32)


def out_last_kernel(peers, *refs):
    hs, (down_ref, o_ref), outs = refs[:peers], refs[peers : peers + 2], refs[peers + 2 :]
    for at in blocks_of(o_ref.shape[1]):
        total = o_ref[:, at]
        for p in range(peers):
            down = part_of(down_ref, p + 1, hs[p].shape[1], at)
            total += jnp.dot(hs[p][...], down, preferred_element_type=F32)
        row = 0
        for out in outs:
            out[:, at] = total[row : row + out.shape[0]].astype(BF16)
            row += out.shape[0]


def mix_kernel(n, high_ref, low_ref, *refs):
    rows, (out_hbm, out_ref, sems) = refs[:n], refs[n:]
    both = jnp.concatenate([high_ref[...], low_ref[...]], axis=1)
    copies = []
    for k, at in enumerate(blocks_of(out_ref.shape[1])):
        x = rows_of(rows, at)
        x = jnp.concatenate([x, x], axis=0)
        out_ref[:, at] = jnp.dot(both, x, preferred_element_type=F32).astype(BF16)
        copies.append(pltpu.make_async_copy(out_ref.at[:, at], out_hbm.at[:, at], sems.at[k]))
        copies[-1].start()
    for copy in copies:
        copy.wait()


def local(tokens, expert_ids, gate_num, gate_weight, up_weight, down_weight):
    cores, depths, peers = (lax.axis_size(a) for a in ("outer", "expert", "inner"))
    groups = cores * depths
    count, width = tokens.shape
    hidden_size = gate_weight.shape[2]
    out_width = down_weight.shape[2]
    slots = groups * CAP
    ids, num = expert_ids.T, gate_num.T
    steps = spread(depths)
    whole = (cores, depths, peers) != PLANNED
    batches = [[0] + steps] if whole else BATCHES
    late, wide, direct = ([], [], []) if whole else (LATE, WIDE, DIRECT)
    soon = [s for s in range(depths) if s not in late]

    pairs = [(c, s) for s in late for c in range(cores)]
    pairs += [(c, s) for c in range(cores) for s in soon]
    parts = [cores * CAP] * len(late) + [CAP] * len(soon) + [len(soon) * CAP] * (cores - 1)
    (tokens,) = call(
        functools.partial(load_kernel, 4),
        [(tokens.shape, BF16)],
        [HBM],
        (LOAD_COST, 2 * tokens.size),
        53.2,
        scratch=[pltpu.SemaphoreType.DMA((4,))],
    )(tokens)
    sent = call(
        functools.partial(fill_kernel, pairs, parts),
        [((p, width), BF16) for p in parts],
        [VMEM, VMEM],
        (2 * slots * count * width, 4 * slots * width),
    )(ids, tokens)
    traded = [turn(x, "outer", c + 1) for c, x in enumerate(sent[len(late) + len(soon) :])]
    chunks = dict(zip(late, sent))
    for k, s in enumerate(soon):
        blocks = [sent[len(late) + k]] + [t[k * CAP : (k + 1) * CAP] for t in traded]
        chunks[s] = jnp.concatenate(blocks, axis=0)
    here, there = {0: chunks[0]}, {}
    for s in steps:
        here[s] = turn(chunks[s], "expert", s)
        if s in late:
            here[s] = exchange(here[s], cores, 1)
        if s in wide:
            there[s] = [turn(chunks[s], "inner", p) for p in range(1, peers)]
            there[s] = [turn(x, "expert", s) for x in there[s]]
    if whole:
        here = {0: jnp.concatenate([here[s] for s in batches[0]], axis=0)}
    for s, x in here.items():
        if s not in wide:
            there[s] = [turn(x, "inner", p) for p in range(1, peers)]

    done = {}
    for batch in batches:
        held = [0] if whole else batch
        n, size = len(held), len(batch) * cores * CAP
        flops = 4 * size * width * hidden_size
        g, u = call(
            functools.partial(in_first_kernel, n),
            [((size, hidden_size), F32)] * 2,
            [VMEM] * (n + 2),
            (flops, 4 * width * hidden_size),
            28,
        )(*[here[s] for s in held], gate_weight, up_weight)
        (hidden,) = call(
            functools.partial(in_last_kernel, n, peers - 1),
            [((size, hidden_size), BF16)],
            [VMEM] * (n * (peers - 1) + 4),
            (flops * (peers - 1), 4 * width * hidden_size * (peers - 1)),
            28,
        )(*[there[s][p] for p in range(peers - 1) for s in held], gate_weight, up_weight, g, u)
        hidden_there = [turn(hidden, "inner", p) for p in range(1, peers)]
        flops = 2 * size * hidden_size * out_width
        (partial,) = call(
            out_first_kernel,
            [((size, out_width), F32)],
            [VMEM, VMEM],
            (flops, 2 * hidden_size * out_width),
            20,
        )(hidden, down_weight)
        outs = list(call(
            functools.partial(out_last_kernel, peers - 1),
            [
                ((size, out_width), BF16)
                for s in batch
                for size in ([CAP] * cores if s in direct else [cores * CAP])
            ],
            [VMEM] * (peers + 1),
            (flops * (peers - 1), 2 * hidden_size * out_width * (peers - 1)),
            20,
        )(*hidden_there, down_weight, partial))
        for s in batch:
            done[s] = [outs.pop(0) for _ in range(cores if s in direct else 1)]

    final, pairs = [], []
    for s in [0] + steps:
        if s in direct:
            for c in range(cores):
                final.append(turn_both(done[s][c], -c, -s))
        else:
            (x,) = done[s]
            if s:
                x = turn(x, "expert", depths - s)
            final.append(exchange(x, cores, -1))
        pairs += [(c, s) for c in range(cores)]

    high, low = call(
        functools.partial(share_kernel, pairs),
        [((count, slots), BF16)] * 2,
        [HBM, HBM],
        (SHARE_COST, 4 * slots * count),
        scratch=[pltpu.VMEM(ids.shape, jnp.int32)] * 2 + [pltpu.SemaphoreType.DMA((2,))],
    )(ids, num)
    (mixed,) = call(
        functools.partial(mix_kernel, len(final)),
        [((count, out_width), BF16)],
        [VMEM] * (2 + len(final)),
        (4 * count * slots * out_width, 4 * count * out_width),
        out_space=HBM,
        scratch=[
            pltpu.VMEM((count, out_width), BF16),
            pltpu.SemaphoreType.DMA((len(blocks_of(out_width)),)),
        ],
    )(high, low, *final)
    return mixed


def solution(mesh):
    placed = (
        P(("parts", "outer", "expert"), "inner"),
        P(("parts", "outer", "expert"), None),
        P(("parts", "outer", "expert"), None),
        P(("outer", "expert"), None, "inner"),
        P(("outer", "expert"), None, "inner"),
        P(("outer", "expert"), None, "inner"),
    )

    step = jax.shard_map(
        local,
        mesh=mesh,
        in_specs=placed,
        out_specs=P(("parts", "outer", "expert"), "inner"),
        check_vma=False,
    )
    if tuple(mesh.shape[a] for a in ("outer", "expert", "inner")) != PLANNED:
        return step
    return step
```

```python
import functools

import jax
import jax.numpy as jnp
from jax import lax
from jax.experimental import pallas as pl
from jax.experimental.pallas import tpu as pltpu
from jax.sharding import PartitionSpec as P


CAP = 16
BATCHES = [[0, 3], [2, 1]]
SHARE_COST = 1e10
LOAD_COST = 3e9
LATE, WIDE, DIRECT = [3], [1], [2, 1]
MIB = 1 << 20
VMEM = pl.BlockSpec(memory_space=pltpu.VMEM)
HBM = pl.BlockSpec(memory_space=pltpu.HBM)
BF16, F32 = jnp.bfloat16, jnp.float32


def call(body, outs, specs, cost, limit=16, out_space=VMEM, scratch=()):
    flops, moved = cost
    return pl.pallas_call(
        body,
        out_shape=[jax.ShapeDtypeStruct(s, d) for s, d in outs],
        in_specs=specs,
        out_specs=[out_space] * len(outs),
        scratch_shapes=scratch,
        compiler_params=pltpu.CompilerParams(vmem_limit_bytes=int(limit * MIB)),
        cost_estimate=pl.CostEstimate(flops=int(flops), bytes_accessed=moved, transcendentals=0),
    )


def turn(x, axis, by):
    size = lax.axis_size(axis)
    return lax.ppermute(x, axis, [(k, (k + by) % size) for k in range(size)])


def turn_both(x, up, along):
    cores, depths = lax.axis_size("outer"), lax.axis_size("expert")
    pairs = [
        (o * depths + z, (o + up) % cores * depths + (z + along) % depths)
        for o in range(cores)
        for z in range(depths)
    ]
    return lax.ppermute(x, ("outer", "expert"), pairs)


def exchange(chunk, cores, way):
    blocks = [chunk[:CAP]]
    for c in range(1, cores):
        blocks.append(turn(chunk[c * CAP : (c + 1) * CAP], "outer", (way * c) % cores))
    return jnp.concatenate(blocks, axis=0)


def spread(order):
    steps = []
    for k in range(1, order):
        for step in (k, order - k):
            if step not in steps and 0 < step < order:
                steps.append(step)
    return steps


def experts(pairs):
    cores, depths = lax.axis_size("outer"), lax.axis_size("expert")
    core, depth = lax.axis_index("outer"), lax.axis_index("expert")
    return [lax.rem(core + c, cores) * depths + lax.rem(depth + s, depths) for c, s in pairs]


def peer_part(p):
    peers = lax.axis_size("inner")
    return lax.rem(lax.axis_index("inner") + peers - p, peers)


def part_of(ref, p, depth, at):
    return ref[0, pl.ds(pl.multiple_of(peer_part(p) * depth, depth), depth), at]


def hits_of(order, ids):
    rows = [jnp.max(jnp.where(ids == e, 1.0, 0.0), axis=0, keepdims=True) for e in order]
    return jnp.concatenate(rows, axis=0)


def places(hits):
    groups, count = hits.shape
    before = lax.broadcasted_iota(jnp.int32, (count, count), 0)
    after = lax.broadcasted_iota(jnp.int32, (count, count), 1)
    earlier = jnp.dot(
        hits.astype(BF16),
        jnp.where(before < after, 1.0, 0.0).astype(BF16),
        preferred_element_type=F32,
    )
    slot = lax.broadcasted_iota(jnp.int32, (groups, CAP, count), 1).astype(F32)
    taken = jnp.where(hits > 0.5, earlier, -1.0)
    return jnp.where(taken[:, None, :] == slot, 1.0, 0.0)


def blocks_of(width, size=256):
    return [slice(at, min(at + size, width)) for at in range(0, width, size)]


def load_kernel(pieces, from_hbm, to_ref, sems):
    size = from_hbm.shape[0] // pieces
    copies = []
    for k in range(pieces):
        at = slice(k * size, (k + 1) * size)
        copies.append(pltpu.make_async_copy(from_hbm.at[at], to_ref.at[at], sems.at[k]))
        copies[-1].start()
    for copy in copies:
        copy.wait()


def fill_kernel(pairs, parts, ids_ref, tokens_ref, *outs):
    order = experts(pairs)
    pick = places(hits_of(order, ids_ref[...]))
    pick = pick.reshape(len(order) * CAP, ids_ref.shape[1]).astype(BF16)
    for at in blocks_of(tokens_ref.shape[1]):
        rows = jnp.dot(pick, tokens_ref[:, at], preferred_element_type=F32).astype(BF16)
        row = 0
        for out, size in zip(outs, parts):
            out[:, at] = rows[row : row + size]
            row += size


def share_kernel(pairs, ids_hbm, num_hbm, high_ref, low_ref, ids_ref, num_ref, sems):
    ids_copy = pltpu.make_async_copy(ids_hbm, ids_ref, sems.at[0])
    num_copy = pltpu.make_async_copy(num_hbm, num_ref, sems.at[1])
    ids_copy.start()
    num_copy.start()
    ids_copy.wait()
    num_copy.wait()
    ids, order = ids_ref[...], experts(pairs)
    groups, count = len(order), ids.shape[1]
    num = num_ref[...].astype(F32)
    live = jnp.where(ids < groups, num, 0.0)
    total = jnp.maximum(jnp.sum(live, axis=0, keepdims=True), 1.0)
    given = [
        jnp.sum(jnp.where(ids == e, num, 0.0), axis=0, keepdims=True) / total for e in order
    ]
    weight = jnp.concatenate(given, axis=0)
    slots = places(hits_of(order, ids)) * weight[:, None, :]
    mix = slots.reshape(groups * CAP, count).T
    high = mix.astype(BF16)
    high_ref[...] = high
    low_ref[...] = (mix - high.astype(F32)).astype(BF16)


def rows_of(refs, at=slice(None)):
    return jnp.concatenate([r[:, at] for r in refs], axis=0)


def filled(x):
    return x if x.shape[0] >= 128 else jnp.concatenate([x, x], axis=0)


def in_first_kernel(n, *refs):
    x, (gate_ref, up_ref, g_ref, u_ref) = rows_of(refs[:n]), refs[n:]
    size, depth = x.shape
    x = filled(x)
    for at in blocks_of(g_ref.shape[1]):
        g_ref[:, at] = jnp.dot(x, part_of(gate_ref, 0, depth, at), preferred_element_type=F32)[:size]
        u_ref[:, at] = jnp.dot(x, part_of(up_ref, 0, depth, at), preferred_element_type=F32)[:size]


def in_last_kernel(n, peers, *refs):
    xs, (gate_ref, up_ref, g_ref, u_ref, h_ref) = refs[: n * peers], refs[n * peers :]
    xs = [rows_of(xs[p * n : (p + 1) * n]) for p in range(peers)]
    size = xs[0].shape[0]
    xs = [filled(x) for x in xs]
    for at in blocks_of(h_ref.shape[1]):
        g, u = g_ref[:, at], u_ref[:, at]
        for p, x in enumerate(xs):
            depth = x.shape[1]
            g += jnp.dot(x, part_of(gate_ref, p + 1, depth, at), preferred_element_type=F32)[:size]
            u += jnp.dot(x, part_of(up_ref, p + 1, depth, at), preferred_element_type=F32)[:size]
        h_ref[:, at] = (g * jax.nn.sigmoid(g) * u).astype(BF16)


def out_first_kernel(h_ref, down_ref, o_ref):
    size, h = h_ref.shape[0], filled(h_ref[...])
    for at in blocks_of(o_ref.shape[1]):
        down = part_of(down_ref, 0, h.shape[1], at)
        o_ref[:, at] = jnp.dot(h, down, preferred_element_type=F32)[:size]


def out_last_kernel(peers, *refs):
    hs, (down_ref, o_ref), outs = refs[:peers], refs[peers : peers + 2], refs[peers + 2 :]
    for at in blocks_of(o_ref.shape[1]):
        total = o_ref[:, at]
        for p in range(peers):
            down = part_of(down_ref, p + 1, hs[p].shape[1], at)
            h = filled(hs[p][...])
            total += jnp.dot(h, down, preferred_element_type=F32)[: total.shape[0]]
        row = 0
        for out in outs:
            out[:, at] = total[row : row + out.shape[0]].astype(BF16)
            row += out.shape[0]


def mix_kernel(n, high_ref, low_ref, *refs):
    rows, (out_hbm, out_ref, sems) = refs[:n], refs[n:]
    both = jnp.concatenate([high_ref[...], low_ref[...]], axis=1)
    copies = []
    for k, at in enumerate(blocks_of(out_ref.shape[1])):
        x = rows_of(rows, at)
        x = jnp.concatenate([x, x], axis=0)
        out_ref[:, at] = jnp.dot(both, x, preferred_element_type=F32).astype(BF16)
        copies.append(pltpu.make_async_copy(out_ref.at[:, at], out_hbm.at[:, at], sems.at[k]))
        copies[-1].start()
    for copy in copies:
        copy.wait()


def local(tokens, expert_ids, gate_num, gate_weight, up_weight, down_weight):
    cores, depths, peers = (lax.axis_size(a) for a in ("outer", "expert", "inner"))
    groups = cores * depths
    count, width = tokens.shape
    hidden_size = gate_weight.shape[2]
    out_width = down_weight.shape[2]
    slots = groups * CAP
    ids, num = expert_ids.T, gate_num.T
    steps = spread(depths)
    whole = depths > 4 or peers > 2
    batches = [[0] + steps] if whole else BATCHES
    late, wide, direct = ([], [], []) if whole else (LATE, WIDE, DIRECT)
    soon = [s for s in range(depths) if s not in late]

    pairs = [(c, s) for s in late for c in range(cores)]
    pairs += [(c, s) for c in range(cores) for s in soon]
    parts = [cores * CAP] * len(late) + [CAP] * len(soon) + [len(soon) * CAP] * (cores - 1)
    (tokens,) = call(
        functools.partial(load_kernel, 4),
        [(tokens.shape, BF16)],
        [HBM],
        (LOAD_COST, 2 * tokens.size),
        53.2,
        scratch=[pltpu.SemaphoreType.DMA((4,))],
    )(tokens)
    sent = call(
        functools.partial(fill_kernel, pairs, parts),
        [((p, width), BF16) for p in parts],
        [VMEM, VMEM],
        (2 * slots * count * width, 4 * slots * width),
    )(ids, tokens)
    traded = [turn(x, "outer", c + 1) for c, x in enumerate(sent[len(late) + len(soon) :])]
    chunks = dict(zip(late, sent))
    for k, s in enumerate(soon):
        blocks = [sent[len(late) + k]] + [t[k * CAP : (k + 1) * CAP] for t in traded]
        chunks[s] = jnp.concatenate(blocks, axis=0)
    here, there = {0: chunks[0]}, {}
    for s in steps:
        here[s] = turn(chunks[s], "expert", s)
        if s in late:
            here[s] = exchange(here[s], cores, 1)
        if s in wide:
            there[s] = [turn(chunks[s], "inner", p) for p in range(1, peers)]
            there[s] = [turn(x, "expert", s) for x in there[s]]
    if whole:
        here = {0: jnp.concatenate([here[s] for s in batches[0]], axis=0)}
    for s, x in here.items():
        if s not in wide:
            there[s] = [turn(x, "inner", p) for p in range(1, peers)]

    done = {}
    for batch in batches:
        held = [0] if whole else batch
        n, size = len(held), len(batch) * cores * CAP
        flops = 4 * size * width * hidden_size
        g, u = call(
            functools.partial(in_first_kernel, n),
            [((size, hidden_size), F32)] * 2,
            [VMEM] * (n + 2),
            (flops, 4 * width * hidden_size),
            28,
        )(*[here[s] for s in held], gate_weight, up_weight)
        (hidden,) = call(
            functools.partial(in_last_kernel, n, peers - 1),
            [((size, hidden_size), BF16)],
            [VMEM] * (n * (peers - 1) + 4),
            (flops * (peers - 1), 4 * width * hidden_size * (peers - 1)),
            28,
        )(*[there[s][p] for p in range(peers - 1) for s in held], gate_weight, up_weight, g, u)
        hidden_there = [turn(hidden, "inner", p) for p in range(1, peers)]
        flops = 2 * size * hidden_size * out_width
        (partial,) = call(
            out_first_kernel,
            [((size, out_width), F32)],
            [VMEM, VMEM],
            (flops, 2 * hidden_size * out_width),
            20,
        )(hidden, down_weight)
        outs = list(call(
            functools.partial(out_last_kernel, peers - 1),
            [
                ((size, out_width), BF16)
                for s in batch
                for size in ([CAP] * cores if s in direct else [cores * CAP])
            ],
            [VMEM] * (peers + 1),
            (flops * (peers - 1), 2 * hidden_size * out_width * (peers - 1)),
            20,
        )(*hidden_there, down_weight, partial))
        for s in batch:
            done[s] = [outs.pop(0) for _ in range(cores if s in direct else 1)]

    final, pairs = [], []
    for s in [0] + steps:
        if s in direct:
            for c in range(cores):
                final.append(turn_both(done[s][c], -c, -s))
        else:
            (x,) = done[s]
            if s:
                x = turn(x, "expert", depths - s)
            final.append(exchange(x, cores, -1))
        pairs += [(c, s) for c in range(cores)]

    high, low = call(
        functools.partial(share_kernel, pairs),
        [((count, slots), BF16)] * 2,
        [HBM, HBM],
        (SHARE_COST, 4 * slots * count),
        scratch=[pltpu.VMEM(ids.shape, jnp.int32)] * 2 + [pltpu.SemaphoreType.DMA((2,))],
    )(ids, num)
    (mixed,) = call(
        functools.partial(mix_kernel, len(final)),
        [((count, out_width), BF16)],
        [VMEM] * (2 + len(final)),
        (4 * count * slots * out_width, 4 * count * out_width),
        out_space=HBM,
        scratch=[
            pltpu.VMEM((count, out_width), BF16),
            pltpu.SemaphoreType.DMA((len(blocks_of(out_width)),)),
        ],
    )(high, low, *final)
    return mixed


def solution(mesh):
    placed = (
        P(("parts", "outer", "expert"), "inner"),
        P(("parts", "outer", "expert"), None),
        P(("parts", "outer", "expert"), None),
        P(("outer", "expert"), None, "inner"),
        P(("outer", "expert"), None, "inner"),
        P(("outer", "expert"), None, "inner"),
    )

    return jax.shard_map(
        local,
        mesh=mesh,
        in_specs=placed,
        out_specs=P(("parts", "outer", "expert"), "inner"),
        check_vma=False,
    )
```
